32 devices in a mesh: groups: 2 (over x), tokens: 16 (over z, y, core).
Axes of the slice: x: 2, y: 2, z: 4, core: 2. Of those that a mesh axis runs over, the one named last changes fastest.
Arguments:
- update_keys: bfloat16 [16384, 2048], P(('groups', 'tokens')), parts along dimension 0, may hold values from -6 to 6
- update_values: bfloat16 [16384, 2048], P(('groups', 'tokens')), parts along dimension 0, may hold values from -6 to 6
- update_rates: float32 [16384, 4], P(('groups', 'tokens')), parts along dimension 0, may hold values from 0.05 to 1
- update_mask: int32 [16384], P(('groups', 'tokens')), parts along dimension 0, may hold values 0 or 1
- fast_weights: bfloat16 [4, 3, 512, 512], replicated, may hold values from -0.25 to 0.25
- step_sizes: float32 [4], replicated, may hold values from 0.02 to 0.08
- target_queries: bfloat16 [4096, 2048], P(('groups', 'tokens')), parts along dimension 0, may hold values from -8 to 8
- target_keys: bfloat16 [4096, 2048], P(('groups', 'tokens')), parts along dimension 0, may hold values from -8 to 8
- target_values: bfloat16 [4096, 2048], P(('groups', 'tokens')), parts along dimension 0, may hold values from -6 to 6
- target_views: int32 [4096], P(('groups', 'tokens')), parts along dimension 0, may hold values from 0 to 15, as said below
Outputs:
- mixed: bfloat16 [4096, 2048], P(('groups', 'tokens')), parts along dimension 0
The draws below stay inside these ranges and needn't reach their ends.
There are 2 independent parts, one for each index of `groups`. The reference program is written for one: setup_inputs(seed, part) draws one part's arguments, and reference() takes and returns one part's arrays. A program takes and returns all parts, laid end to end along the dimension named above; an argument that names none is the same for every part. Nothing has to cross between parts.
Inputs may be any that keep to these rules, and one draw needn't show every extreme that they name: `target_views`: every view id names exactly 128 rows. Owner o holds view o; of the 128 rows of one device, either none or exactly 16 belong to the view of one owner.
All inputs are finite; a program needn't handle non-finite values. No bound on the sum of `update_mask` on one device may be relied on, other than what follows from the above.
Results may differ from the reference program's by a relative error of at most 0.0083.
Values may be sent and summed in bfloat16 or wider, within the bound.
A program may use at most 128 MiB of HBM per device.

```python
import math
import jax
import jax.numpy as jnp
from jax import lax

HEADS = 4
DH = 512
VIEW_ROWS = 128
UPD_DEV = 512
VIEWS_DEV = 1
WIDTH = 2048
TGT_DEV = 128
CAP = 16
UPD_ROWS = 8192
TGT_ROWS = 2048
VIEWS = 16
N_TOKENS = 16


def view_layout(key):
    dev_count = TGT_ROWS // TGT_DEV
    half_count = dev_count // 2
    offsets = jax.random.permutation(jax.random.fold_in(key, 11), dev_count)[:half_count]
    source_dev = jnp.arange(dev_count, dtype=jnp.int32)[:, None]
    dest_pairs = (source_dev + offsets[None, :].astype(jnp.int32)) % dev_count
    dest_dev = jnp.repeat(dest_pairs, CAP, axis=1)
    incoming = jnp.broadcast_to(jnp.arange(TGT_DEV, dtype=jnp.int32)[None, :], (dev_count, TGT_DEV))
    arrival = jax.vmap(lambda sub_key: jax.random.permutation(sub_key, TGT_DEV))(jax.random.split(jax.random.fold_in(key, 12), dev_count))
    local_view = arrival[dest_dev, incoming].astype(jnp.int32) // VIEW_ROWS
    view_ids = dest_dev * VIEWS_DEV + local_view
    shuffle = jax.vmap(lambda sub_key: jax.random.permutation(sub_key, TGT_DEV))(jax.random.split(jax.random.fold_in(key, 13), dev_count))
    view_ids = jnp.take_along_axis(view_ids, shuffle.astype(jnp.int32), axis=1)
    return view_ids.reshape(-1).astype(jnp.int32)


def draw_target_views(key, part):
    return view_layout(key)


def drawn_pair(key):
    shape = (TGT_ROWS, WIDTH)
    queries = jnp.clip(jax.random.normal(jax.random.fold_in(key, 27), shape, jnp.float32), -4.0, 4.0)
    keys_out = jnp.clip(jax.random.normal(jax.random.fold_in(key, 28), shape, jnp.float32), -4.0, 4.0)
    return (queries, keys_out)


def draw_target_queries(key, part):
    return drawn_pair(key)[0].astype(jnp.bfloat16)


def draw_target_keys(key, part):
    return drawn_pair(key)[1].astype(jnp.bfloat16)


def touch_ends(result, stream_key, smallest, high):
    index_at = [jax.random.randint(jax.random.fold_in(stream_key, axis), (), 0, length) for axis, length in enumerate(result.shape)]
    main_axis = result.shape.index(max(result.shape))
    neighbour = index_at[:main_axis] + [(index_at[main_axis] + 1) % result.shape[main_axis]] + index_at[main_axis + 1:]
    return result.at[tuple(index_at)].set(smallest).at[tuple(neighbour)].set(high)


def raised(entries, key, source, target, shards_of, factor):
    def block_of(axis_at):
        return (jnp.arange(entries.shape[axis_at]) // (entries.shape[axis_at] // shards_of)).reshape((-1,) + (1,) * (entries.ndim - 1 - axis_at))

    near = jax.random.permutation(key, shards_of)[block_of(target)]
    far = (block_of(target) + shards_of // 2) % shards_of
    return jnp.where((block_of(source) == near) | (block_of(source) == far), factor * entries, entries)


def block_scale(key, shape, cuts, smallest, largest):
    def one(axis_at, shards_of):
        draws = jax.random.uniform(jax.random.fold_in(jax.random.fold_in(key, 6), axis_at), (shards_of,), jnp.float32, smallest / len(cuts), largest / len(cuts))
        return jnp.repeat(jnp.exp(draws), shape[axis_at] // shards_of).reshape((-1,) + (1,) * (len(shape) - axis_at - 1))

    level = one(*cuts[0])
    for cut in cuts[1:]:
        level = level * one(*cut)
    return level


def bell_draw(stream_key, dims, width, reach, pieces=(), held_as=jnp.bfloat16):
    entries = jax.random.normal(stream_key, dims, jnp.float32) * width
    if len(pieces) > 0:
        entries = block_scale(stream_key, dims, pieces, -0.22, 0.18) * entries
    return jnp.clip(entries, min=-reach, max=reach).astype(held_as)


def heavy_noise(stream_key, dims, deviation, limit, pieces, heavy, held_as=jnp.bfloat16):
    values = deviation * jax.random.normal(stream_key, dims, jnp.float32)
    if pieces:
        values = values * block_scale(stream_key, dims, pieces, -0.22, 0.18)
    return jnp.clip(raised(values, jax.random.fold_in(stream_key, 3), *heavy), -limit, limit).astype(held_as)


def setup_inputs(seed: int = 0, part: int = 0) -> dict:
    key_list = jax.random.split(jax.random.key(seed), 11)
    own_keys = jax.random.split(jax.random.fold_in(key_list[10], part), 11)
    update_keys = heavy_noise(own_keys[0], (UPD_ROWS, WIDTH), 1.0, 6.0, ((0, 16),), (0, 1, 16, 2.0))
    update_values = bell_draw(own_keys[1], (UPD_ROWS, WIDTH), 1.0, 6.0, ((0, 16),))
    update_rates = jnp.clip(jnp.exp(math.log(1.0) - 2.9957323 * jax.random.uniform(own_keys[2], (UPD_ROWS, HEADS), jnp.float32) ** block_scale(own_keys[2], (UPD_ROWS, HEADS), ((0, 16),), -0.2, 0.2)), 0.05, 1.0)
    update_mask = touch_ends((jax.random.randint(own_keys[3], (UPD_ROWS,), 0, 4) < 3).astype(jnp.int32), jax.random.fold_in(own_keys[3], 1), 0, 1)
    fast_weights = bell_draw(key_list[4], (HEADS, 3, DH, DH), DH ** -0.5, 0.25)
    step_sizes = jnp.clip(jnp.exp(jax.random.uniform(key_list[5], (HEADS,), jnp.float32, math.log(0.02), math.log(0.08))), 0.02, 0.08)
    target_queries = draw_target_queries(jax.random.fold_in(jax.random.fold_in(key_list[10], part), 71), part)
    target_keys = draw_target_keys(jax.random.fold_in(jax.random.fold_in(key_list[10], part), 71), part)
    target_values = bell_draw(own_keys[8], (TGT_ROWS, WIDTH), 1.0, 6.0, ((0, 16),))
    target_views = draw_target_views(jax.random.fold_in(jax.random.fold_in(key_list[10], part), 71), part)
    return dict(update_keys=update_keys, update_values=update_values, update_rates=update_rates, update_mask=update_mask, fast_weights=fast_weights, step_sizes=step_sizes, target_queries=target_queries, target_keys=target_keys, target_values=target_values, target_views=target_views)


epsilon = 1e-05
highest = lax.Precision.HIGHEST

def rounded(values):
    return lax.optimization_barrier(values.astype(jnp.bfloat16)).astype(jnp.float32)

def swish_parts(pre_gate):
    sigma = jax.nn.sigmoid(pre_gate)
    return (pre_gate * sigma, sigma * (1.0 + pre_gate * (1.0 - sigma)))

def row_normalize(matrix):
    return matrix * lax.rsqrt(lax.optimization_barrier(jnp.mean(matrix * matrix, axis=-1, keepdims=True)) + epsilon)

def reference(update_keys, update_values, update_rates, update_mask, fast_weights, step_sizes, target_queries, target_keys, target_values, target_views):
    weights = fast_weights.astype(jnp.float32)
    keep_rates = update_mask.astype(jnp.float32)[:, None] * update_rates

    def accumulate(block_index, grad_sum):
        first_row = (block_index * UPD_DEV).astype(jnp.int32)
        key_rows = lax.dynamic_slice_in_dim(update_keys, first_row, UPD_DEV, 0).astype(jnp.float32).reshape(UPD_DEV, HEADS, DH)
        value_rows = lax.dynamic_slice_in_dim(update_values, first_row, UPD_DEV, 0).astype(jnp.float32).reshape(UPD_DEV, HEADS, DH)
        rate_rows = lax.dynamic_slice_in_dim(keep_rates, first_row, UPD_DEV, 0)
        target_grad = rounded(-rate_rows[:, :, None] * value_rows)
        pre_gate = jnp.einsum('rhi,hij->rhj', key_rows, weights[:, 0], precision=highest)
        pre_up = jnp.einsum('rhi,hij->rhj', key_rows, weights[:, 1], precision=highest)
        activated, slope = swish_parts(pre_gate)
        hidden = rounded(activated * pre_up)
        back = jnp.einsum('rho,hjo->rhj', target_grad, weights[:, 2], precision=highest)
        grad_gate = rounded(back * pre_up * slope)
        grad_up = rounded(back * activated)
        gate_term = jnp.einsum('rhi,rhj->hij', key_rows, grad_gate, precision=highest)
        up_term = jnp.einsum('rhi,rhj->hij', key_rows, grad_up, precision=highest)
        down_term = jnp.einsum('rhj,rho->hjo', hidden, target_grad, precision=highest)
        return grad_sum + jnp.stack([gate_term, up_term, down_term], axis=1)
    gradient = lax.fori_loop(0, N_TOKENS, accumulate, jnp.zeros((HEADS, 3, DH, DH), jnp.float32))
    fresh = rounded(weights - step_sizes[:, None, None, None] * row_normalize(gradient))
    view_hit = (target_views[:, None] == jnp.arange(VIEWS, dtype=jnp.int32)[None, :]).astype(jnp.int32)
    within_view = lax.optimization_barrier(jnp.sum(view_hit * (jnp.cumsum(view_hit, axis=0) - 1), axis=1))
    position = (target_views * VIEW_ROWS + within_view).astype(jnp.int32)
    arranged = [jnp.zeros_like(source_rows).at[position].set(source_rows) for source_rows in (target_queries, target_keys, target_values)]
    query_rows = arranged[0].astype(jnp.float32).reshape(TGT_ROWS, HEADS, DH)
    pre_gate = jnp.einsum('rhi,hij->rhj', query_rows, fresh[:, 0], precision=highest)
    pre_up = jnp.einsum('rhi,hij->rhj', query_rows, fresh[:, 1], precision=highest)
    activated, slope = swish_parts(pre_gate)
    target_hidden = rounded(activated * pre_up)
    fast_out = jnp.einsum('rhj,hjo->rho', target_hidden, fresh[:, 2], precision=highest)
    normed = row_normalize(fast_out)
    view_shape = (VIEWS, VIEW_ROWS, HEADS, DH)
    view_queries = arranged[0].astype(jnp.float32).reshape(view_shape)
    view_keys = arranged[1].astype(jnp.float32).reshape(view_shape)
    view_values = arranged[2].astype(jnp.float32).reshape(view_shape)
    scores = jnp.einsum('vqhd,vkhd->vhqk', view_queries, view_keys, precision=highest) * DH ** (-0.5)
    probs = rounded(jax.nn.softmax(scores, axis=-1))
    attended = jnp.einsum('vhqk,vkhd->vqhd', probs, view_values, precision=highest).reshape(TGT_ROWS, HEADS, DH)
    return (normed + attended).reshape(TGT_ROWS, WIDTH).astype(jnp.bfloat16)
```

```python
import functools
import math

import jax
import jax.numpy as jnp
from jax import lax
from jax.experimental import pallas as pl
from jax.experimental.pallas import tpu as pltpu
from jax.sharding import PartitionSpec as P

EPS = 1e-05
VIEW_ROWS = 128
MESH = pl.DeviceIdType.MESH
F32 = jnp.float32
BF16 = jnp.bfloat16


def remote(src, dst, send_sem, recv_sem, peer):
    return pltpu.make_async_remote_copy(
        src_ref=src,
        dst_ref=dst,
        send_sem=send_sem,
        recv_sem=recv_sem,
        device_id={"tokens": peer},
        device_id_type=MESH,
    )


def exchange_kernel(
    n,
    heads,
    keys_ref,
    values_ref,
    rates_ref,
    weights_ref,
    steps_ref,
    packed_ref,
    meta_ref,
    fresh_ref,
    got_ref,
    got_meta_ref,
    grad,
    core_out,
    core_in,
    side_out,
    side_in,
    up_out,
    up_in,
    down_out,
    down_in,
    a2a_send,
    a2a_recv,
    meta_send,
    meta_recv,
    pair_send,
    pair_recv,
    chain_send,
    chain_recv,
    spread_send,
    spread_recv,
):
    width = weights_ref.shape[-1]
    quads = n // heads
    piece = 3 * width // quads
    slots = packed_ref.shape[1] // quads
    me = lax.axis_index("tokens")
    quad = me // heads
    head = me % heads
    core = head % 2
    side = head // 2
    core_peer = me + 1 - 2 * core
    side_peer = me + 2 - 4 * side

    barrier = pltpu.get_barrier_semaphore()
    for step in range(1, n):
        pl.semaphore_signal(
            barrier, inc=1, device_id={"tokens": (me + step) % n}, device_id_type=MESH
        )
    pl.semaphore_wait(barrier, n - 1)

    def block_copy(step):
        peer = (me + step) % n
        rows = pl.ds(pl.multiple_of((peer // heads) * slots, slots), slots)
        columns = pl.ds(pl.multiple_of((peer % heads) * width, width), width)
        return remote(
            packed_ref.at[:, rows, columns],
            got_ref.at[me],
            a2a_send.at[step],
            a2a_recv.at[step],
            peer,
        )

    def meta_copy(step):
        peer = (me + step) % n
        return remote(
            meta_ref, got_meta_ref.at[me], meta_send.at[step], meta_recv.at[step], peer
        )

    for step in range(1, n):
        meta_copy(step).start()
    for step in range(1, n):
        block_copy(step).start()
    got_meta_ref[me] = meta_ref[...]
    got_ref[me] = packed_ref[
        :,
        pl.ds(pl.multiple_of(quad * slots, slots), slots),
        pl.ds(pl.multiple_of(head * width, width), width),
    ]

    def core_copy(slot):
        return remote(
            core_out.at[slot], core_in.at[slot], pair_send.at[slot], pair_recv.at[slot], core_peer
        )

    side_copy = remote(side_out, side_in, pair_send.at[2], pair_recv.at[2], side_peer)

    def one_head(turn, carry):
        on_side = jnp.where(turn < 2, 1 - side, side)
        on_core = jnp.where(turn % 2 == 0, 1 - core, core)
        now = on_side * 2 + on_core
        columns = pl.ds(pl.multiple_of(now * width, width), width)
        key_rows = keys_ref[:, columns]
        rates = rates_ref[...]
        lanes = lax.broadcasted_iota(jnp.int32, rates.shape, 1)
        rate = jnp.sum(jnp.where(lanes == now, rates, 0.0), axis=1, keepdims=True)
        target_grad = (-rate * values_ref[:, columns].astype(F32)).astype(BF16)
        pre_gate = jnp.dot(key_rows, weights_ref[now, 0], preferred_element_type=F32)
        pre_up = jnp.dot(key_rows, weights_ref[now, 1], preferred_element_type=F32)
        back = lax.dot_general(
            target_grad,
            weights_ref[now, 2],
            (((1,), (1,)), ((), ())),
            preferred_element_type=F32,
        )
        sigma = jax.nn.sigmoid(pre_gate)
        activated = pre_gate * sigma
        hidden = (activated * pre_up).astype(BF16)
        grad_gate = (back * pre_up * sigma * (1.0 + pre_gate * (1.0 - sigma))).astype(BF16)
        grad_up = (back * activated).astype(BF16)
        over_rows = (((0,), (0,)), ((), ()))
        grad[0:width] = lax.dot_general(
            key_rows, grad_gate, over_rows, preferred_element_type=F32
        )
        grad[width : 2 * width] = lax.dot_general(
            key_rows, grad_up, over_rows, preferred_element_type=F32
        )
        grad[2 * width : 3 * width] = lax.dot_general(
            hidden, target_grad, over_rows, preferred_element_type=F32
        )

        @pl.when(turn == 0)
        def _():
            core_out[0] = grad[...].astype(BF16)
            core_copy(0).start()

        @pl.when(turn == 1)
        def _():
            core_copy(0).wait_recv()
            side_out[...] = (grad[...] + core_in[0].astype(F32)).astype(BF16)
            side_copy.start()

        @pl.when(turn == 2)
        def _():
            core_out[1] = grad[...].astype(BF16)
            core_copy(1).start()

        return carry

    lax.fori_loop(0, 4, one_head, 0)
    core_copy(1).wait_recv()
    side_copy.wait_recv()

    def rows_of(index):
        return pl.ds(index * piece, piece)

    def own_part(rows):
        return grad[rows, :] + core_in[1, rows, :].astype(F32) + side_in[rows, :].astype(F32)

    def up_copy(index):
        return remote(
            up_out.at[index],
            up_in.at[index],
            chain_send.at[0, index],
            chain_recv.at[0, index],
            me + heads,
        )

    def down_copy(index):
        return remote(
            down_out.at[index],
            down_in.at[index],
            chain_send.at[1, index],
            chain_recv.at[1, index],
            me - heads,
        )

    for turn in range(quads - 1):
        high = quads - 1 - turn
        low = turn

        @pl.when(quad == 0)
        def _():
            up_out[high] = own_part(rows_of(high)).astype(BF16)
            up_copy(high).start()

        @pl.when(quad == quads - 1)
        def _():
            down_out[low] = own_part(rows_of(low)).astype(BF16)
            down_copy(low).start()

        @pl.when((quad > 0) & (quad < high))
        def _():
            up_copy(high).wait_recv()
            up_out[high] = (own_part(rows_of(high)) + up_in[high].astype(F32)).astype(BF16)
            up_copy(high).start()

        @pl.when((quad < quads - 1) & (quad > low))
        def _():
            down_copy(low).wait_recv()
            down_out[low] = (own_part(rows_of(low)) + down_in[low].astype(F32)).astype(BF16)
            down_copy(low).start()

    mine = pl.ds(pl.multiple_of(quad * piece, piece), piece)
    grad[mine, :] = own_part(mine)

    @pl.when(quad > 0)
    def _():
        up_copy(quad).wait_recv()
        grad[mine, :] += up_in[quad].astype(F32)

    @pl.when(quad < quads - 1)
    def _():
        down_copy(quad).wait_recv()
        grad[mine, :] += down_in[quad].astype(F32)

    total = grad[mine, :]
    scaled = total * lax.rsqrt(jnp.mean(total * total, axis=-1, keepdims=True) + EPS)
    first = quad * piece
    block = math.gcd(piece, width)
    for part in range(piece // block):
        start = first + part * block
        old = weights_ref[
            head, start // width, pl.ds(pl.multiple_of(start % width, block), block), :
        ]
        fresh_ref[quad, part * block : (part + 1) * block, :] = (
            old.astype(F32) - steps_ref[head] * scaled[part * block : (part + 1) * block, :]
        ).astype(BF16)

    def spread_copy(way, index):
        return remote(
            fresh_ref.at[index],
            fresh_ref.at[index],
            spread_send.at[way, index],
            spread_recv.at[index],
            me + heads if way == 0 else me - heads,
        )

    @pl.when(quad < quads - 1)
    def _():
        spread_copy(0, quad).start()

    @pl.when(quad > 0)
    def _():
        spread_copy(1, quad).start()

    for hop in range(1, quads):

        @pl.when(quad - hop >= 0)
        def _():
            index = quad - hop
            spread_copy(0, index).wait_recv()

            @pl.when(quad < quads - 1)
            def _():
                spread_copy(0, index).start()

        @pl.when(quad + hop < quads)
        def _():
            index = quad + hop
            spread_copy(1, index).wait_recv()

            @pl.when(quad > 0)
            def _():
                spread_copy(1, index).start()

    core_copy(0).wait_send()
    core_copy(1).wait_send()
    side_copy.wait_send()
    for index in range(quads):

        @pl.when(quad < index)
        def _():
            up_copy(index).wait_send()

        @pl.when(quad > index)
        def _():
            down_copy(index).wait_send()

        @pl.when((index <= quad) & (quad < quads - 1))
        def _():
            spread_copy(0, index).wait_send()

        @pl.when((index >= quad) & (quad > 0))
        def _():
            spread_copy(1, index).wait_send()

    for step in range(1, n):
        meta_copy(step).wait()
        block_copy(step).wait()


def exchange(keys, values, rates, weights, steps, packed, meta):
    n = lax.axis_size("tokens")
    heads = weights.shape[0]
    width = weights.shape[-1]
    quads = n // heads
    piece = 3 * width // quads
    slots = packed.shape[1] // quads
    rows = keys.shape[0]
    vmem = pl.BlockSpec(memory_space=pltpu.VMEM)
    smem = pl.BlockSpec(memory_space=pltpu.SMEM)
    dma = pltpu.SemaphoreType.DMA
    whole = (3 * width, width)
    parts = (quads, piece, width)
    return pl.pallas_call(
        functools.partial(exchange_kernel, n, heads),
        out_shape=(
            jax.ShapeDtypeStruct(parts, BF16),
            jax.ShapeDtypeStruct((n, 3, slots, width), BF16),
            jax.ShapeDtypeStruct((n,) + meta.shape, jnp.int32),
        ),
        in_specs=[vmem, vmem, vmem, vmem, smem, vmem, vmem],
        out_specs=(vmem, vmem, vmem),
        scratch_shapes=[
            pltpu.VMEM(whole, F32),
            pltpu.VMEM((2,) + whole, BF16),
            pltpu.VMEM((2,) + whole, BF16),
            pltpu.VMEM(whole, BF16),
            pltpu.VMEM(whole, BF16),
            pltpu.VMEM(parts, BF16),
            pltpu.VMEM(parts, BF16),
            pltpu.VMEM(parts, BF16),
            pltpu.VMEM(parts, BF16),
            dma((n,)),
            dma((n,)),
            dma((n,)),
            dma((n,)),
            dma((3,)),
            dma((3,)),
            dma((2, quads)),
            dma((2, quads)),
            dma((2, quads)),
            dma((quads,)),
        ],
        compiler_params=pltpu.CompilerParams(
            collective_id=0, has_side_effects=True, vmem_limit_bytes=63 * 1024 * 1024
        ),
    )(keys, values, rates, weights, steps, packed, meta)


def pack_rows(queries, keys, values, views, n):
    rows = views.shape[0]
    capacity = 2 * rows // n
    hits = (views[:, None] // (rows // VIEW_ROWS) == jnp.arange(n, dtype=jnp.int32)[None, :]).astype(
        jnp.int32
    )
    before = jnp.tril(jnp.ones((rows, rows), BF16), -1)
    rank = jnp.sum(
        hits * jnp.dot(before, hits.astype(BF16), preferred_element_type=F32).astype(jnp.int32),
        axis=1,
    )
    slot = (views // (rows // VIEW_ROWS)) * capacity + rank
    pick = (jnp.arange(n * capacity, dtype=jnp.int32)[:, None] == slot[None, :]).astype(BF16)
    packed = jnp.stack(
        [
            jnp.dot(pick, array, preferred_element_type=F32).astype(BF16)
            for array in (queries, keys, values)
        ]
    )
    counts = jnp.sum(hits, axis=0)
    lanes = -(-n // 128) * 128
    meta = jnp.broadcast_to(jnp.pad(counts, (0, lanes - n))[None, :], (8, lanes))
    return packed, meta


def on_device(
    update_keys,
    update_values,
    update_rates,
    update_mask,
    fast_weights,
    step_sizes,
    target_queries,
    target_keys,
    target_values,
    target_views,
):
    n = lax.axis_size("tokens")
    heads = fast_weights.shape[0]
    width = fast_weights.shape[2]
    me = lax.axis_index("tokens")
    packed, meta = pack_rows(target_queries, target_keys, target_values, target_views, n)
    rates = update_rates * update_mask.astype(F32)[:, None]
    fresh, got, got_meta = exchange(
        update_keys, update_values, rates, fast_weights, step_sizes, packed, meta
    )
    fresh = fresh.reshape(3, width, width)
    rows = target_views.shape[0]
    capacity = 2 * rows // n
    counts = lax.dynamic_slice_in_dim(got_meta[:, 0, :], (me // heads) * heads, heads, 1)
    first = jnp.cumsum(counts, axis=0) - counts
    inside = jnp.arange(capacity, dtype=jnp.int32)
    place_at = jnp.where(
        inside[None, None, :] < counts[:, :, None], first[:, :, None] + inside[None, None, :], -1
    )
    place_at = jnp.transpose(place_at, (1, 0, 2)).reshape(heads, n * capacity)
    place = (
        jnp.arange(rows, dtype=jnp.int32)[None, :, None] == place_at[:, None, :]
    ).astype(BF16)
    got = got.reshape(n, 3, heads, capacity, width)
    got = jnp.transpose(got, (1, 2, 0, 3, 4)).reshape(3, heads, n * capacity, width)
    arranged = jnp.einsum("vrs,cvsd->cvrd", place, got, preferred_element_type=F32).astype(BF16)
    scores = (
        jnp.einsum("vqd,vkd->vqk", arranged[0], arranged[1], preferred_element_type=F32)
        * width ** (-0.5)
    )
    probs = jax.nn.softmax(scores, axis=-1).astype(BF16)
    attended = jnp.einsum("vqk,vkd->vqd", probs, arranged[2], preferred_element_type=F32)
    query_rows = arranged[0].reshape(heads * rows, width)
    pre_gate = jnp.dot(query_rows, fresh[0], preferred_element_type=F32)
    pre_up = jnp.dot(query_rows, fresh[1], preferred_element_type=F32)
    hidden = (pre_gate * jax.nn.sigmoid(pre_gate) * pre_up).astype(BF16)
    fast_out = jnp.dot(hidden, fresh[2], preferred_element_type=F32)
    normed = fast_out * lax.rsqrt(jnp.mean(fast_out * fast_out, axis=-1, keepdims=True) + EPS)
    mixed = (normed.reshape(heads, rows, width) + attended).astype(BF16)
    groups = [[first + i for i in range(heads)] for first in range(0, n, heads)]
    swapped = lax.all_to_all(
        mixed, "tokens", split_axis=0, concat_axis=0, axis_index_groups=groups, tiled=True
    )
    return jnp.transpose(swapped, (1, 0, 2)).reshape(rows, heads * width)


def solution(mesh):
    rows = P(("groups", "tokens"), None)
    flat = P(("groups", "tokens"))
    return jax.shard_map(
        on_device,
        mesh=mesh,
        in_specs=(rows, rows, rows, flat, P(), P(), rows, rows, rows, flat),
        out_specs=rows,
        check_vma=False,
    )
```

```python
import functools
import math

import jax
import jax.numpy as jnp
import numpy as np
from jax import lax
from jax.experimental import pallas as pl
from jax.experimental.pallas import tpu as pltpu
from jax.sharding import PartitionSpec as P

EPS = 1e-05
MESH = pl.DeviceIdType.MESH
F32 = jnp.float32
BF16 = jnp.bfloat16


def remote(src, dst, send_sem, recv_sem, peer):
    return pltpu.make_async_remote_copy(
        src_ref=src,
        dst_ref=dst,
        send_sem=send_sem,
        recv_sem=recv_sem,
        device_id={"tokens": peer},
        device_id_type=MESH,
    )


def exchange_kernel(
    n,
    heads,
    keys_ref,
    values_ref,
    rates_ref,
    weights_ref,
    steps_ref,
    queries_ref,
    view_keys_ref,
    view_values_ref,
    views_ref,
    lanes_ref,
    out_ref,
    packed_ref,
    meta_ref,
    fresh_ref,
    got_ref,
    got_meta_ref,
    query_rows,
    attended,
    mixed,
    grad,
    core_out,
    core_in,
    side_out,
    side_in,
    up_out,
    up_in,
    down_out,
    down_in,
    a2a_send,
    a2a_recv,
    meta_send,
    meta_recv,
    pair_send,
    pair_recv,
    chain_send,
    chain_recv,
    spread_send,
    spread_recv,
    out_send,
    out_recv,
):
    width = weights_ref.shape[-1]
    rows = queries_ref.shape[0]
    quads = n // heads
    piece = 3 * width // quads
    slots = packed_ref.shape[1] // quads
    capacity = slots // heads
    me = lax.axis_index("tokens")
    quad = me // heads
    head = me % heads
    core = head % 2
    side = head // 2
    core_peer = me + 1 - 2 * core
    side_peer = me + 2 - 4 * side

    barrier = pltpu.get_barrier_semaphore()
    for step in range(1, n):
        pl.semaphore_signal(
            barrier, inc=1, device_id={"tokens": (me + step) % n}, device_id_type=MESH
        )

    owner = views_ref[0:1, :]
    hits = lax.broadcasted_iota(jnp.int32, (meta_ref.shape[1], rows), 0) == owner
    hits = hits.astype(F32).astype(BF16)
    earlier = (
        lax.broadcasted_iota(jnp.int32, (rows, rows), 0)
        < lax.broadcasted_iota(jnp.int32, (rows, rows), 1)
    ).astype(F32).astype(BF16)
    before = jnp.dot(hits, earlier, preferred_element_type=F32)
    rank = jnp.sum(hits.astype(F32) * before, axis=0, keepdims=True).astype(jnp.int32)
    meta_ref[...] = lax.dot_general(
        jnp.ones((meta_ref.shape[0], rows), BF16),
        hits,
        (((1,), (1,)), ((), ())),
        preferred_element_type=F32,
    )
    pick = (
        lax.broadcasted_iota(jnp.int32, (n * capacity, rows), 0) == owner * capacity + rank
    ).astype(F32).astype(BF16)
    for index, array in enumerate((queries_ref, view_keys_ref, view_values_ref)):
        packed_ref[index] = jnp.dot(pick, array[...], preferred_element_type=F32).astype(BF16)

    pl.semaphore_wait(barrier, n - 1)

    near = [step for step in range(1, n) if step % heads < 2]
    cross = [step for step in range(1, n) if step % heads >= 2]
    early = cross[len(cross) // 2 :] + near[::-1]
    late = cross[: len(cross) // 2][::-1]

    def peer_of(step):
        place, total = me, 0
        unit = 1
        while unit < n:
            bit = place % 2
            total = total + unit * ((1 - bit) if (step // unit) % 2 else bit)
            place = place // 2
            unit *= 2
        return total

    def block_copy(step):
        peer = peer_of(step)
        rows = pl.ds(pl.multiple_of((peer // heads) * slots, slots), slots)
        columns = pl.ds(pl.multiple_of((peer % heads) * width, width), width)
        return remote(
            packed_ref.at[:, rows, columns],
            got_ref.at[me],
            a2a_send.at[step],
            a2a_recv.at[step],
            peer,
        )

    def meta_copy(step):
        peer = peer_of(step)
        return remote(
            meta_ref, got_meta_ref.at[me], meta_send.at[step], meta_recv.at[step], peer
        )

    for step in range(1, n):
        meta_copy(step).start()
    for step in early:
        block_copy(step).start()
    got_meta_ref[me] = meta_ref[...]
    got_ref[me] = packed_ref[
        :,
        pl.ds(pl.multiple_of(quad * slots, slots), slots),
        pl.ds(pl.multiple_of(head * width, width), width),
    ]

    def core_copy(slot):
        return remote(
            core_out.at[slot], core_in.at[slot], pair_send.at[slot], pair_recv.at[slot], core_peer
        )

    side_copy = remote(side_out, side_in, pair_send.at[2], pair_recv.at[2], side_peer)

    def one_head(turn, carry):
        on_side = jnp.where(turn < 2, 1 - side, side)
        on_core = jnp.where(turn % 2 == 0, 1 - core, core)
        now = on_side * 2 + on_core
        columns = pl.ds(pl.multiple_of(now * width, width), width)
        key_rows = keys_ref[:, columns]
        rates = rates_ref[...]
        lanes = lax.broadcasted_iota(jnp.int32, rates.shape, 1)
        rate = jnp.sum(jnp.where(lanes == now, rates, 0.0), axis=1, keepdims=True)
        target_grad = (-rate * values_ref[:, columns].astype(F32)).astype(BF16)
        pre_gate = jnp.dot(key_rows, weights_ref[now, 0], preferred_element_type=F32)
        pre_up = jnp.dot(key_rows, weights_ref[now, 1], preferred_element_type=F32)
        back = lax.dot_general(
            target_grad,
            weights_ref[now, 2],
            (((1,), (1,)), ((), ())),
            preferred_element_type=F32,
        )
        sigma = jax.nn.sigmoid(pre_gate)
        activated = pre_gate * sigma
        hidden = (activated * pre_up).astype(BF16)
        grad_gate = (back * pre_up * sigma * (1.0 + pre_gate * (1.0 - sigma))).astype(BF16)
        grad_up = (back * activated).astype(BF16)
        over_rows = (((0,), (0,)), ((), ()))
        grad[0:width] = lax.dot_general(
            key_rows, grad_gate, over_rows, preferred_element_type=F32
        )
        grad[width : 2 * width] = lax.dot_general(
            key_rows, grad_up, over_rows, preferred_element_type=F32
        )
        grad[2 * width : 3 * width] = lax.dot_general(
            hidden, target_grad, over_rows, preferred_element_type=F32
        )

        @pl.when(turn == 0)
        def _():
            core_out[0] = grad[...].astype(BF16)
            core_copy(0).start()

        @pl.when(turn == 1)
        def _():
            core_copy(0).wait_recv()
            side_out[...] = (grad[...] + core_in[0].astype(F32)).astype(BF16)
            side_copy.start()
            for step in late:
                block_copy(step).start()

        @pl.when(turn == 2)
        def _():
            core_out[1] = grad[...].astype(BF16)
            core_copy(1).start()

        return carry

    lax.fori_loop(0, 4, one_head, 0)
    core_copy(1).wait_recv()
    side_copy.wait_recv()

    def rows_of(index):
        return pl.ds(index * piece, piece)

    def own_part(rows):
        return grad[rows, :] + core_in[1, rows, :].astype(F32) + side_in[rows, :].astype(F32)

    def up_copy(index):
        return remote(
            up_out.at[index],
            up_in.at[index],
            chain_send.at[0, index],
            chain_recv.at[0, index],
            me + heads,
        )

    def down_copy(index):
        return remote(
            down_out.at[index],
            down_in.at[index],
            chain_send.at[1, index],
            chain_recv.at[1, index],
            me - heads,
        )

    for turn in range(quads - 1):
        high = quads - 1 - turn
        low = turn

        @pl.when(quad == 0)
        def _():
            up_out[high] = own_part(rows_of(high)).astype(BF16)
            up_copy(high).start()

        @pl.when(quad == quads - 1)
        def _():
            down_out[low] = own_part(rows_of(low)).astype(BF16)
            down_copy(low).start()

        @pl.when((quad > 0) & (quad < high))
        def _():
            up_copy(high).wait_recv()
            up_out[high] = (own_part(rows_of(high)) + up_in[high].astype(F32)).astype(BF16)
            up_copy(high).start()

        @pl.when((quad < quads - 1) & (quad > low))
        def _():
            down_copy(low).wait_recv()
            down_out[low] = (own_part(rows_of(low)) + down_in[low].astype(F32)).astype(BF16)
            down_copy(low).start()

    mine = pl.ds(pl.multiple_of(quad * piece, piece), piece)
    grad[mine, :] = own_part(mine)

    @pl.when(quad > 0)
    def _():
        up_copy(quad).wait_recv()
        grad[mine, :] += up_in[quad].astype(F32)

    @pl.when(quad < quads - 1)
    def _():
        down_copy(quad).wait_recv()
        grad[mine, :] += down_in[quad].astype(F32)

    total = grad[mine, :]
    scaled = total * lax.rsqrt(jnp.mean(total * total, axis=-1, keepdims=True) + EPS)
    first = quad * piece
    block = math.gcd(piece, width)
    for part in range(piece // block):
        start = first + part * block
        old = weights_ref[
            head, start // width, pl.ds(pl.multiple_of(start % width, block), block), :
        ]
        fresh_ref[quad, part * block : (part + 1) * block, :] = (
            old.astype(F32) - steps_ref[head] * scaled[part * block : (part + 1) * block, :]
        ).astype(BF16)

    def spread_copy(way, index):
        return remote(
            fresh_ref.at[index],
            fresh_ref.at[index],
            spread_send.at[way, index],
            spread_recv.at[index],
            me + heads if way == 0 else me - heads,
        )

    @pl.when(quad < quads - 1)
    def _():
        spread_copy(0, quad).start()

    @pl.when(quad > 0)
    def _():
        spread_copy(1, quad).start()

    for step in range(1, n):
        meta_copy(step).wait()
        block_copy(step).wait()
    lane_source, lane_view, lane_slot = (lanes_ref[i : i + 1, :] for i in range(3))
    lane_count = lanes_ref.shape[1]
    counts = got_meta_ref[:, 0, :].astype(BF16)
    sources = lax.broadcasted_iota(jnp.int32, (n, lane_count), 0)
    over_source = (((0,), (0,)), ((), ()))
    same = (sources == lane_source).astype(F32).astype(BF16)
    lower = (sources < lane_source).astype(F32).astype(BF16)
    owners = lax.broadcasted_iota(jnp.int32, (meta_ref.shape[1], lane_count), 0)
    wanted = owners == lane_view + quad * heads

    def lane_sum(table):
        found = lax.dot_general(counts, table, over_source, preferred_element_type=F32)
        return jnp.sum(jnp.where(wanted, found, 0.0), axis=0, keepdims=True).astype(jnp.int32)

    place_at = jnp.where(
        lane_slot < lane_sum(same), lane_view * rows + lane_sum(lower) + lane_slot, -1
    )
    place = (
        lax.broadcasted_iota(jnp.int32, (heads * rows, lane_count), 0) == place_at
    ).astype(F32).astype(BF16)
    arranged = [
        jnp.dot(
            place, got_ref[:, i].reshape(lane_count, width), preferred_element_type=F32
        ).astype(BF16)
        for i in range(3)
    ]
    for view in range(heads):
        part = slice(view * rows, (view + 1) * rows)
        scores = lax.dot_general(
            arranged[0][part], arranged[1][part], (((1,), (1,)), ((), ())),
            preferred_element_type=F32,
        ) * width ** (-0.5)
        powers = jnp.exp(scores - jnp.max(scores, axis=-1, keepdims=True))
        probs = (powers / jnp.sum(powers, axis=-1, keepdims=True)).astype(BF16)
        attended[part] = jnp.dot(probs, arranged[2][part], preferred_element_type=F32)
    query_rows[...] = arranged[0]

    for hop in range(1, quads):

        @pl.when(quad - hop >= 0)
        def _():
            index = quad - hop
            spread_copy(0, index).wait_recv()

            @pl.when(quad < quads - 1)
            def _():
                spread_copy(0, index).start()

        @pl.when(quad + hop < quads)
        def _():
            index = quad + hop
            spread_copy(1, index).wait_recv()

            @pl.when(quad > 0)
            def _():
                spread_copy(1, index).start()

    fresh = fresh_ref[...].reshape(3 * width, width)
    pre_gate = jnp.dot(query_rows[...], fresh[0:width], preferred_element_type=F32)
    pre_up = jnp.dot(query_rows[...], fresh[width : 2 * width], preferred_element_type=F32)
    target_hidden = (pre_gate * jax.nn.sigmoid(pre_gate) * pre_up).astype(BF16)
    fast_out = jnp.dot(target_hidden, fresh[2 * width :], preferred_element_type=F32)
    normed = fast_out * lax.rsqrt(jnp.mean(fast_out * fast_out, axis=-1, keepdims=True) + EPS)
    mixed[...] = (normed + attended[...]).astype(BF16).reshape(mixed.shape)
    own_columns = pl.ds(pl.multiple_of(head * width, width), width)

    def out_copy(step):
        view = (head + step) % heads
        return remote(
            mixed.at[view],
            out_ref.at[:, own_columns],
            out_send.at[step],
            out_recv.at[step],
            quad * heads + view,
        )

    for step in range(1, heads):
        out_copy(step).start()
    out_ref[:, own_columns] = mixed[head]
    for step in range(1, heads):
        out_copy(step).wait()

    core_copy(0).wait_send()
    core_copy(1).wait_send()
    side_copy.wait_send()
    for index in range(quads):

        @pl.when(quad < index)
        def _():
            up_copy(index).wait_send()

        @pl.when(quad > index)
        def _():
            down_copy(index).wait_send()

        @pl.when((index <= quad) & (quad < quads - 1))
        def _():
            spread_copy(0, index).wait_send()

        @pl.when((index >= quad) & (quad > 0))
        def _():
            spread_copy(1, index).wait_send()


def exchange(keys, values, rates, weights, steps, queries, view_keys, view_values, views):
    n = lax.axis_size("tokens")
    heads = weights.shape[0]
    width = weights.shape[-1]
    rows = queries.shape[0]
    quads = n // heads
    piece = 3 * width // quads
    capacity = 2 * rows // n
    slots = heads * capacity
    owner_lanes = -(-n // 128) * 128
    lane = np.arange(n * slots)
    lanes = np.zeros((8, n * slots), np.int32)
    lanes[0] = lane // slots
    lanes[1] = lane % slots // capacity
    lanes[2] = lane % capacity
    vmem = pl.BlockSpec(memory_space=pltpu.VMEM)
    smem = pl.BlockSpec(memory_space=pltpu.SMEM)
    dma = pltpu.SemaphoreType.DMA
    whole = (3 * width, width)
    parts = (quads, piece, width)
    return pl.pallas_call(
        functools.partial(exchange_kernel, n, heads),
        out_shape=jax.ShapeDtypeStruct((rows, heads * width), BF16),
        in_specs=[vmem, vmem, vmem, vmem, smem] + [vmem] * 5,
        out_specs=vmem,
        scratch_shapes=[
            pltpu.VMEM((3, n * capacity, heads * width), BF16),
            pltpu.VMEM((8, owner_lanes), F32),
            pltpu.VMEM(parts, BF16),
            pltpu.VMEM((n, 3, slots, width), BF16),
            pltpu.VMEM((n, 8, owner_lanes), F32),
            pltpu.VMEM((heads * rows, width), BF16),
            pltpu.VMEM((heads * rows, width), F32),
            pltpu.VMEM((heads, rows, width), BF16),
            pltpu.VMEM(whole, F32),
            pltpu.VMEM((2,) + whole, BF16),
            pltpu.VMEM((2,) + whole, BF16),
            pltpu.VMEM(whole, BF16),
            pltpu.VMEM(whole, BF16),
            pltpu.VMEM(parts, BF16),
            pltpu.VMEM(parts, BF16),
            pltpu.VMEM(parts, BF16),
            pltpu.VMEM(parts, BF16),
            dma((n,)),
            dma((n,)),
            dma((n,)),
            dma((n,)),
            dma((3,)),
            dma((3,)),
            dma((2, quads)),
            dma((2, quads)),
            dma((2, quads)),
            dma((quads,)),
            dma((heads,)),
            dma((heads,)),
        ],
        compiler_params=pltpu.CompilerParams(
            collective_id=0, has_side_effects=True, vmem_limit_bytes=63 * 1024 * 1024
        ),
    )(keys, values, rates, weights, steps, queries, view_keys, view_values, views, jnp.asarray(lanes))


def on_device(
    update_keys,
    update_values,
    update_rates,
    update_mask,
    fast_weights,
    step_sizes,
    target_queries,
    target_keys,
    target_values,
    target_views,
):
    rates = update_rates * update_mask.astype(F32)[:, None]
    return exchange(
        update_keys,
        update_values,
        rates,
        fast_weights,
        step_sizes,
        target_queries,
        target_keys,
        target_values,
        target_views[None, :],
    )


def solution(mesh):
    rows = P(("groups", "tokens"), None)
    flat = P(("groups", "tokens"))
    return jax.shard_map(
        on_device,
        mesh=mesh,
        in_specs=(rows, rows, rows, flat, P(), P(), rows, rows, rows, flat),
        out_specs=rows,
        check_vma=False,
    )
```

```python
import functools
import math

import jax
import jax.numpy as jnp
import numpy as np
from jax import lax
from jax.experimental import pallas as pl
from jax.experimental.pallas import tpu as pltpu
from jax.sharding import PartitionSpec as P

EPS = 1e-05
MESH = pl.DeviceIdType.MESH
F32 = jnp.float32
BF16 = jnp.bfloat16


def remote(src, dst, send_sem, recv_sem, peer):
    return pltpu.make_async_remote_copy(
        src_ref=src,
        dst_ref=dst,
        send_sem=send_sem,
        recv_sem=recv_sem,
        device_id={"tokens": peer},
        device_id_type=MESH,
    )


def exchange_kernel(
    n,
    heads,
    keys_ref,
    values_ref,
    rates_ref,
    weights_ref,
    steps_ref,
    queries_ref,
    view_keys_ref,
    view_values_ref,
    views_ref,
    lanes_ref,
    out_ref,
    packed_ref,
    meta_ref,
    fresh_ref,
    got_ref,
    got_meta_ref,
    query_rows,
    attended,
    mixed,
    grad,
    core_out,
    core_in,
    side_out,
    side_in,
    up_out,
    up_in,
    down_out,
    down_in,
    a2a_send,
    a2a_recv,
    meta_send,
    meta_recv,
    pair_send,
    pair_recv,
    chain_send,
    chain_recv,
    spread_send,
    spread_recv,
    out_send,
    out_recv,
):
    width = weights_ref.shape[-1]
    rows = queries_ref.shape[0]
    quads = n // heads
    piece = 3 * width // quads
    slots = packed_ref.shape[1] // quads
    capacity = slots // heads
    me = lax.axis_index("tokens")
    quad = me // heads
    head = me % heads
    core = head % 2
    side = head // 2
    core_peer = me + 1 - 2 * core
    side_peer = me + 2 - 4 * side

    barrier = pltpu.get_barrier_semaphore()
    for step in range(1, n):
        pl.semaphore_signal(
            barrier, inc=1, device_id={"tokens": (me + step) % n}, device_id_type=MESH
        )

    owner = views_ref[0:1, :]
    hits = lax.broadcasted_iota(jnp.int32, (meta_ref.shape[1], rows), 0) == owner
    hits = hits.astype(F32).astype(BF16)
    earlier = (
        lax.broadcasted_iota(jnp.int32, (rows, rows), 0)
        < lax.broadcasted_iota(jnp.int32, (rows, rows), 1)
    ).astype(F32).astype(BF16)
    before = jnp.dot(hits, earlier, preferred_element_type=F32)
    rank = jnp.sum(hits.astype(F32) * before, axis=0, keepdims=True).astype(jnp.int32)
    meta_ref[...] = lax.dot_general(
        jnp.ones((meta_ref.shape[0], rows), BF16),
        hits,
        (((1,), (1,)), ((), ())),
        preferred_element_type=F32,
    )
    pick = (
        lax.broadcasted_iota(jnp.int32, (n * capacity, rows), 0) == owner * capacity + rank
    ).astype(F32).astype(BF16)
    for index, array in enumerate((queries_ref, view_keys_ref, view_values_ref)):
        packed_ref[index] = jnp.dot(pick, array[...], preferred_element_type=F32).astype(BF16)

    pl.semaphore_wait(barrier, n - 1)

    near = [step for step in range(1, n) if step % heads < 2]
    cross = [step for step in range(1, n) if step % heads >= 2]
    early = near[::-1]
    late = cross[::-1]

    def peer_of(step):
        place, total = me, 0
        unit = 1
        while unit < n:
            bit = place % 2
            total = total + unit * ((1 - bit) if (step // unit) % 2 else bit)
            place = place // 2
            unit *= 2
        return total

    def block_copy(step):
        peer = peer_of(step)
        rows = pl.ds(pl.multiple_of((peer // heads) * slots, slots), slots)
        columns = pl.ds(pl.multiple_of((peer % heads) * width, width), width)
        return remote(
            packed_ref.at[:, rows, columns],
            got_ref.at[me],
            a2a_send.at[step],
            a2a_recv.at[step],
            peer,
        )

    def meta_copy(step):
        peer = peer_of(step)
        return remote(
            meta_ref, got_meta_ref.at[me], meta_send.at[step], meta_recv.at[step], peer
        )

    for step in range(1, n):
        meta_copy(step).start()
    for step in early:
        block_copy(step).start()
    got_meta_ref[me] = meta_ref[...]
    got_ref[me] = packed_ref[
        :,
        pl.ds(pl.multiple_of(quad * slots, slots), slots),
        pl.ds(pl.multiple_of(head * width, width), width),
    ]

    def core_copy(slot):
        return remote(
            core_out.at[slot], core_in.at[slot], pair_send.at[slot], pair_recv.at[slot], core_peer
        )

    side_copy = remote(side_out, side_in, pair_send.at[2], pair_recv.at[2], side_peer)

    def one_head(turn, carry):
        on_side = jnp.where(turn < 2, 1 - side, side)
        on_core = jnp.where(turn % 2 == 0, 1 - core, core)
        now = on_side * 2 + on_core
        columns = pl.ds(pl.multiple_of(now * width, width), width)
        key_rows = keys_ref[:, columns]
        rates = rates_ref[...]
        lanes = lax.broadcasted_iota(jnp.int32, rates.shape, 1)
        rate = jnp.sum(jnp.where(lanes == now, rates, 0.0), axis=1, keepdims=True)
        target_grad = (-rate * values_ref[:, columns].astype(F32)).astype(BF16)
        pre_gate = jnp.dot(key_rows, weights_ref[now, 0], preferred_element_type=F32)
        pre_up = jnp.dot(key_rows, weights_ref[now, 1], preferred_element_type=F32)
        back = lax.dot_general(
            target_grad,
            weights_ref[now, 2],
            (((1,), (1,)), ((), ())),
            preferred_element_type=F32,
        )
        sigma = jax.nn.sigmoid(pre_gate)
        activated = pre_gate * sigma
        hidden = (activated * pre_up).astype(BF16)
        grad_gate = (back * pre_up * sigma * (1.0 + pre_gate * (1.0 - sigma))).astype(BF16)
        grad_up = (back * activated).astype(BF16)
        over_rows = (((0,), (0,)), ((), ()))
        grad[0:width] = lax.dot_general(
            key_rows, grad_gate, over_rows, preferred_element_type=F32
        )
        grad[width : 2 * width] = lax.dot_general(
            key_rows, grad_up, over_rows, preferred_element_type=F32
        )
        grad[2 * width : 3 * width] = lax.dot_general(
            hidden, target_grad, over_rows, preferred_element_type=F32
        )

        @pl.when(turn == 0)
        def _():
            core_out[0] = grad[...].astype(BF16)
            core_copy(0).start()

        @pl.when(turn == 1)
        def _():
            core_copy(0).wait_recv()
            side_out[...] = (grad[...] + core_in[0].astype(F32)).astype(BF16)
            side_copy.start()
            for step in late:
                block_copy(step).start()

        @pl.when(turn == 2)
        def _():
            core_out[1] = grad[...].astype(BF16)
            core_copy(1).start()

        return carry

    lax.fori_loop(0, 4, one_head, 0)
    core_copy(1).wait_recv()
    side_copy.wait_recv()

    def rows_of(index):
        return pl.ds(index * piece, piece)

    def own_part(rows):
        return grad[rows, :] + core_in[1, rows, :].astype(F32) + side_in[rows, :].astype(F32)

    def up_copy(index):
        return remote(
            up_out.at[index],
            up_in.at[index],
            chain_send.at[0, index],
            chain_recv.at[0, index],
            me + heads,
        )

    def down_copy(index):
        return remote(
            down_out.at[index],
            down_in.at[index],
            chain_send.at[1, index],
            chain_recv.at[1, index],
            me - heads,
        )

    def send_up(index):
        @pl.when(quad == 0)
        def _():
            up_out[index] = own_part(rows_of(index)).astype(BF16)
            up_copy(index).start()

        @pl.when((quad > 0) & (quad < index))
        def _():
            up_copy(index).wait_recv()
            up_out[index] = (own_part(rows_of(index)) + up_in[index].astype(F32)).astype(BF16)
            up_copy(index).start()

    def send_down(index):
        @pl.when(quad == quads - 1)
        def _():
            down_out[index] = own_part(rows_of(index)).astype(BF16)
            down_copy(index).start()

        @pl.when((quad < quads - 1) & (quad > index))
        def _():
            down_copy(index).wait_recv()
            down_out[index] = (own_part(rows_of(index)) + down_in[index].astype(F32)).astype(BF16)
            down_copy(index).start()

    @pl.when(2 * quad < quads)
    def _():
        for turn in range(quads - 1):
            send_up(quads - 1 - turn)
            send_down(turn)

    @pl.when(2 * quad >= quads)
    def _():
        for turn in range(quads - 1):
            send_down(turn)
            send_up(quads - 1 - turn)

    mine = pl.ds(pl.multiple_of(quad * piece, piece), piece)
    grad[mine, :] = own_part(mine)

    @pl.when(quad > 0)
    def _():
        up_copy(quad).wait_recv()
        grad[mine, :] += up_in[quad].astype(F32)

    @pl.when(quad < quads - 1)
    def _():
        down_copy(quad).wait_recv()
        grad[mine, :] += down_in[quad].astype(F32)

    total = grad[mine, :]
    scaled = total * lax.rsqrt(jnp.mean(total * total, axis=-1, keepdims=True) + EPS)
    first = quad * piece
    block = math.gcd(piece, width)
    for part in range(piece // block):
        start = first + part * block
        old = weights_ref[
            head, start // width, pl.ds(pl.multiple_of(start % width, block), block), :
        ]
        fresh_ref[quad, part * block : (part + 1) * block, :] = (
            old.astype(F32) - steps_ref[head] * scaled[part * block : (part + 1) * block, :]
        ).astype(BF16)

    def spread_copy(way, index):
        return remote(
            fresh_ref.at[index],
            fresh_ref.at[index],
            spread_send.at[way, index],
            spread_recv.at[index],
            me + heads if way == 0 else me - heads,
        )

    @pl.when(quad < quads - 1)
    def _():
        spread_copy(0, quad).start()

    @pl.when(quad > 0)
    def _():
        spread_copy(1, quad).start()

    for step in range(1, n):
        meta_copy(step).wait()
        block_copy(step).wait()
    lane_source, lane_view, lane_slot = (lanes_ref[i : i + 1, :] for i in range(3))
    lane_count = lanes_ref.shape[1]
    counts = got_meta_ref[:, 0, :].astype(BF16)
    sources = lax.broadcasted_iota(jnp.int32, (n, lane_count), 0)
    over_source = (((0,), (0,)), ((), ()))
    same = (sources == lane_source).astype(F32).astype(BF16)
    lower = (sources < lane_source).astype(F32).astype(BF16)
    owners = lax.broadcasted_iota(jnp.int32, (meta_ref.shape[1], lane_count), 0)
    wanted = owners == lane_view + quad * heads

    def lane_sum(table):
        found = lax.dot_general(counts, table, over_source, preferred_element_type=F32)
        return jnp.sum(jnp.where(wanted, found, 0.0), axis=0, keepdims=True).astype(jnp.int32)

    place_at = jnp.where(
        lane_slot < lane_sum(same), lane_view * rows + lane_sum(lower) + lane_slot, -1
    )
    place = (
        lax.broadcasted_iota(jnp.int32, (heads * rows, lane_count), 0) == place_at
    ).astype(F32).astype(BF16)
    arranged = [
        jnp.dot(
            place, got_ref[:, i].reshape(lane_count, width), preferred_element_type=F32
        ).astype(BF16)
        for i in range(3)
    ]
    for view in range(heads):
        part = slice(view * rows, (view + 1) * rows)
        scores = lax.dot_general(
            arranged[0][part], arranged[1][part], (((1,), (1,)), ((), ())),
            preferred_element_type=F32,
        ) * width ** (-0.5)
        powers = jnp.exp(scores - jnp.max(scores, axis=-1, keepdims=True))
        probs = (powers / jnp.sum(powers, axis=-1, keepdims=True)).astype(BF16)
        attended[part] = jnp.dot(probs, arranged[2][part], preferred_element_type=F32)
    query_rows[...] = arranged[0]

    for hop in range(1, quads):

        @pl.when(quad - hop >= 0)
        def _():
            index = quad - hop
            spread_copy(0, index).wait_recv()

            @pl.when(quad < quads - 1)
            def _():
                spread_copy(0, index).start()

        @pl.when(quad + hop < quads)
        def _():
            index = quad + hop
            spread_copy(1, index).wait_recv()

            @pl.when(quad > 0)
            def _():
                spread_copy(1, index).start()

    fresh = fresh_ref[...].reshape(3 * width, width)
    pre_gate = jnp.dot(query_rows[...], fresh[0:width], preferred_element_type=F32)
    pre_up = jnp.dot(query_rows[...], fresh[width : 2 * width], preferred_element_type=F32)
    target_hidden = (pre_gate * jax.nn.sigmoid(pre_gate) * pre_up).astype(BF16)
    fast_out = jnp.dot(target_hidden, fresh[2 * width :], preferred_element_type=F32)
    normed = fast_out * lax.rsqrt(jnp.mean(fast_out * fast_out, axis=-1, keepdims=True) + EPS)
    mixed[...] = (normed + attended[...]).astype(BF16).reshape(mixed.shape)
    own_columns = pl.ds(pl.multiple_of(head * width, width), width)

    def out_copy(step):
        view = (head + step) % heads
        return remote(
            mixed.at[view],
            out_ref.at[:, own_columns],
            out_send.at[step],
            out_recv.at[step],
            quad * heads + view,
        )

    for step in range(1, heads):
        out_copy(step).start()
    out_ref[:, own_columns] = mixed[head]
    for step in range(1, heads):
        out_copy(step).wait()

    core_copy(0).wait_send()
    core_copy(1).wait_send()
    side_copy.wait_send()
    for index in range(quads):

        @pl.when(quad < index)
        def _():
            up_copy(index).wait_send()

        @pl.when(quad > index)
        def _():
            down_copy(index).wait_send()

        @pl.when((index <= quad) & (quad < quads - 1))
        def _():
            spread_copy(0, index).wait_send()

        @pl.when((index >= quad) & (quad > 0))
        def _():
            spread_copy(1, index).wait_send()


def exchange(keys, values, rates, weights, steps, queries, view_keys, view_values, views):
    n = lax.axis_size("tokens")
    heads = weights.shape[0]
    width = weights.shape[-1]
    rows = queries.shape[0]
    quads = n // heads
    piece = 3 * width // quads
    capacity = 2 * rows // n
    slots = heads * capacity
    owner_lanes = -(-n // 128) * 128
    lane = np.arange(n * slots)
    lanes = np.zeros((8, n * slots), np.int32)
    lanes[0] = lane // slots
    lanes[1] = lane % slots // capacity
    lanes[2] = lane % capacity
    vmem = pl.BlockSpec(memory_space=pltpu.VMEM)
    smem = pl.BlockSpec(memory_space=pltpu.SMEM)
    dma = pltpu.SemaphoreType.DMA
    whole = (3 * width, width)
    parts = (quads, piece, width)
    return pl.pallas_call(
        functools.partial(exchange_kernel, n, heads),
        out_shape=jax.ShapeDtypeStruct((rows, heads * width), BF16),
        in_specs=[vmem, vmem, vmem, vmem, smem] + [vmem] * 5,
        out_specs=vmem,
        scratch_shapes=[
            pltpu.VMEM((3, n * capacity, heads * width), BF16),
            pltpu.VMEM((8, owner_lanes), F32),
            pltpu.VMEM(parts, BF16),
            pltpu.VMEM((n, 3, slots, width), BF16),
            pltpu.VMEM((n, 8, owner_lanes), F32),
            pltpu.VMEM((heads * rows, width), BF16),
            pltpu.VMEM((heads * rows, width), F32),
            pltpu.VMEM((heads, rows, width), BF16),
            pltpu.VMEM(whole, F32),
            pltpu.VMEM((2,) + whole, BF16),
            pltpu.VMEM((2,) + whole, BF16),
            pltpu.VMEM(whole, BF16),
            pltpu.VMEM(whole, BF16),
            pltpu.VMEM(parts, BF16),
            pltpu.VMEM(parts, BF16),
            pltpu.VMEM(parts, BF16),
            pltpu.VMEM(parts, BF16),
            dma((n,)),
            dma((n,)),
            dma((n,)),
            dma((n,)),
            dma((3,)),
            dma((3,)),
            dma((2, quads)),
            dma((2, quads)),
            dma((2, quads)),
            dma((quads,)),
            dma((heads,)),
            dma((heads,)),
        ],
        compiler_params=pltpu.CompilerParams(
            collective_id=0, has_side_effects=True, vmem_limit_bytes=63 * 1024 * 1024
        ),
    )(keys, values, rates, weights, steps, queries, view_keys, view_values, views, jnp.asarray(lanes))


def on_device(
    update_keys,
    update_values,
    update_rates,
    update_mask,
    fast_weights,
    step_sizes,
    target_queries,
    target_keys,
    target_values,
    target_views,
):
    rates = update_rates * update_mask.astype(F32)[:, None]
    return exchange(
        update_keys,
        update_values,
        rates,
        fast_weights,
        step_sizes,
        target_queries,
        target_keys,
        target_values,
        target_views[None, :],
    )


def solution(mesh):
    rows = P(("groups", "tokens"), None)
    flat = P(("groups", "tokens"))
    return jax.shard_map(
        on_device,
        mesh=mesh,
        in_specs=(rows, rows, rows, flat, P(), P(), rows, rows, rows, flat),
        out_specs=rows,
        check_vma=False,
    )
```

```python
import functools
import math

import jax
import jax.numpy as jnp
import numpy as np
from jax import lax
from jax.experimental import pallas as pl
from jax.experimental.pallas import tpu as pltpu
from jax.sharding import PartitionSpec as P

EPS = 1e-05
MESH = pl.DeviceIdType.MESH
F32 = jnp.float32
BF16 = jnp.bfloat16


def remote(src, dst, send_sem, recv_sem, peer):
    return pltpu.make_async_remote_copy(
        src_ref=src,
        dst_ref=dst,
        send_sem=send_sem,
        recv_sem=recv_sem,
        device_id={"tokens": peer},
        device_id_type=MESH,
    )


def exchange_kernel(
    n,
    heads,
    keys_ref,
    values_ref,
    rates_ref,
    weights_ref,
    steps_ref,
    queries_ref,
    view_keys_ref,
    view_values_ref,
    views_ref,
    lanes_ref,
    out_ref,
    packed_ref,
    meta_ref,
    fresh_ref,
    got_ref,
    got_meta_ref,
    query_rows,
    attended,
    mixed,
    grad,
    core_out,
    core_in,
    side_out,
    side_in,
    up_out,
    up_in,
    down_out,
    down_in,
    a2a_send,
    a2a_recv,
    meta_send,
    meta_recv,
    pair_send,
    pair_recv,
    side_send,
    side_recv,
    chain_send,
    chain_recv,
    spread_send,
    spread_recv,
    out_send,
    out_recv,
):
    width = weights_ref.shape[-1]
    rows = queries_ref.shape[0]
    quads = n // heads
    piece = 3 * width // quads
    slots = packed_ref.shape[1] // quads
    capacity = slots // heads
    me = lax.axis_index("tokens")
    quad = me // heads
    head = me % heads
    core = head % 2
    side = head // 2
    core_peer = me + 1 - 2 * core
    side_peer = me + 2 - 4 * side

    barrier = pltpu.get_barrier_semaphore()
    for step in range(1, n):
        pl.semaphore_signal(
            barrier, inc=1, device_id={"tokens": (me + step) % n}, device_id_type=MESH
        )

    owner = views_ref[0:1, :]
    hits = lax.broadcasted_iota(jnp.int32, (meta_ref.shape[1], rows), 0) == owner
    hits = hits.astype(F32).astype(BF16)
    earlier = (
        lax.broadcasted_iota(jnp.int32, (rows, rows), 0)
        < lax.broadcasted_iota(jnp.int32, (rows, rows), 1)
    ).astype(F32).astype(BF16)
    before = jnp.dot(hits, earlier, preferred_element_type=F32)
    rank = jnp.sum(hits.astype(F32) * before, axis=0, keepdims=True).astype(jnp.int32)
    meta_ref[...] = lax.dot_general(
        jnp.ones((meta_ref.shape[0], rows), BF16),
        hits,
        (((1,), (1,)), ((), ())),
        preferred_element_type=F32,
    )
    pick = (
        lax.broadcasted_iota(jnp.int32, (n * capacity, rows), 0) == owner * capacity + rank
    ).astype(F32).astype(BF16)
    for index, array in enumerate((queries_ref, view_keys_ref, view_values_ref)):
        packed_ref[index] = jnp.dot(pick, array[...], preferred_element_type=F32).astype(BF16)

    pl.semaphore_wait(barrier, n - 1)

    near = [step for step in range(1, n) if step % heads < 2]
    cross = [step for step in range(1, n) if step % heads >= 2]
    early = near[::-1]
    late = cross

    def peer_of(step):
        place, total = me, 0
        unit = 1
        while unit < n:
            bit = place % 2
            total = total + unit * ((1 - bit) if (step // unit) % 2 else bit)
            place = place // 2
            unit *= 2
        return total

    def block_copy(step):
        peer = peer_of(step)
        rows = pl.ds(pl.multiple_of((peer // heads) * slots, slots), slots)
        columns = pl.ds(pl.multiple_of((peer % heads) * width, width), width)
        return remote(
            packed_ref.at[:, rows, columns],
            got_ref.at[me],
            a2a_send.at[step],
            a2a_recv.at[step],
            peer,
        )

    def meta_copy(step):
        peer = peer_of(step)
        return remote(
            meta_ref, got_meta_ref.at[me], meta_send.at[step], meta_recv.at[step], peer
        )

    for step in range(1, n):
        meta_copy(step).start()
    for step in early:
        block_copy(step).start()
    got_meta_ref[me] = meta_ref[...]
    got_ref[me] = packed_ref[
        :,
        pl.ds(pl.multiple_of(quad * slots, slots), slots),
        pl.ds(pl.multiple_of(head * width, width), width),
    ]

    def core_copy(slot):
        return remote(
            core_out.at[slot], core_in.at[slot], pair_send.at[slot], pair_recv.at[slot], core_peer
        )

    def side_copy(index):
        part = pl.ds(index * piece, piece)
        return remote(
            side_out.at[part, :],
            side_in.at[part, :],
            side_send.at[index],
            side_recv.at[index],
            side_peer,
        )

    falling = list(range(quads))[::-1]
    rising = falling[::-1]

    def mixed_order(first, second):
        both = [index for pair in zip(first, second) for index in pair]
        return list(dict.fromkeys(both))

    side_orders = (
        (quad == 0, falling),
        (quad == quads - 1, rising),
        ((quad > 0) & (2 * quad < quads), mixed_order(falling, rising)),
        ((quad < quads - 1) & (2 * quad >= quads), mixed_order(rising, falling)),
    )

    def one_head(turn, carry):
        on_side = jnp.where(turn < 2, 1 - side, side)
        on_core = jnp.where(turn % 2 == 0, 1 - core, core)
        now = on_side * 2 + on_core
        columns = pl.ds(pl.multiple_of(now * width, width), width)
        key_rows = keys_ref[:, columns]
        rates = rates_ref[...]
        lanes = lax.broadcasted_iota(jnp.int32, rates.shape, 1)
        rate = jnp.sum(jnp.where(lanes == now, rates, 0.0), axis=1, keepdims=True)
        target_grad = (-rate * values_ref[:, columns].astype(F32)).astype(BF16)
        pre_gate = jnp.dot(key_rows, weights_ref[now, 0], preferred_element_type=F32)
        pre_up = jnp.dot(key_rows, weights_ref[now, 1], preferred_element_type=F32)
        back = lax.dot_general(
            target_grad,
            weights_ref[now, 2],
            (((1,), (1,)), ((), ())),
            preferred_element_type=F32,
        )
        sigma = jax.nn.sigmoid(pre_gate)
        activated = pre_gate * sigma
        hidden = (activated * pre_up).astype(BF16)
        grad_gate = (back * pre_up * sigma * (1.0 + pre_gate * (1.0 - sigma))).astype(BF16)
        grad_up = (back * activated).astype(BF16)
        over_rows = (((0,), (0,)), ((), ()))
        grad[0:width] = lax.dot_general(
            key_rows, grad_gate, over_rows, preferred_element_type=F32
        )
        grad[width : 2 * width] = lax.dot_general(
            key_rows, grad_up, over_rows, preferred_element_type=F32
        )
        grad[2 * width : 3 * width] = lax.dot_general(
            hidden, target_grad, over_rows, preferred_element_type=F32
        )

        @pl.when(turn == 0)
        def _():
            core_out[0] = grad[...].astype(BF16)
            core_copy(0).start()

        @pl.when(turn == 1)
        def _():
            core_copy(0).wait_recv()
            side_out[...] = (grad[...] + core_in[0].astype(F32)).astype(BF16)
            for chosen, order in side_orders:

                @pl.when(chosen)
                def _(order=order):
                    for index in order:
                        side_copy(index).start()

            for step in late:
                block_copy(step).start()

        @pl.when(turn == 2)
        def _():
            core_out[1] = grad[...].astype(BF16)
            core_copy(1).start()

        return carry

    lax.fori_loop(0, 4, one_head, 0)
    core_copy(1).wait_recv()

    def rows_of(index):
        return pl.ds(index * piece, piece)

    def own_part(index, rows):
        side_copy(index).wait_recv()
        return grad[rows, :] + core_in[1, rows, :].astype(F32) + side_in[rows, :].astype(F32)

    def up_copy(index):
        return remote(
            up_out.at[index],
            up_in.at[index],
            chain_send.at[0, index],
            chain_recv.at[0, index],
            me + heads,
        )

    def down_copy(index):
        return remote(
            down_out.at[index],
            down_in.at[index],
            chain_send.at[1, index],
            chain_recv.at[1, index],
            me - heads,
        )

    def send_up(index):
        @pl.when(quad == 0)
        def _():
            up_out[index] = own_part(index, rows_of(index)).astype(BF16)
            up_copy(index).start()

        @pl.when((quad > 0) & (quad < index))
        def _():
            up_copy(index).wait_recv()
            up_out[index] = (own_part(index, rows_of(index)) + up_in[index].astype(F32)).astype(BF16)
            up_copy(index).start()

    def send_down(index):
        @pl.when(quad == quads - 1)
        def _():
            down_out[index] = own_part(index, rows_of(index)).astype(BF16)
            down_copy(index).start()

        @pl.when((quad < quads - 1) & (quad > index))
        def _():
            down_copy(index).wait_recv()
            down_out[index] = (own_part(index, rows_of(index)) + down_in[index].astype(F32)).astype(BF16)
            down_copy(index).start()

    @pl.when(2 * quad < quads)
    def _():
        for turn in range(quads - 1):
            send_up(quads - 1 - turn)
            send_down(turn)

    @pl.when(2 * quad >= quads)
    def _():
        for turn in range(quads - 1):
            send_down(turn)
            send_up(quads - 1 - turn)

    mine = pl.ds(pl.multiple_of(quad * piece, piece), piece)
    grad[mine, :] = own_part(quad, mine)

    @pl.when(quad > 0)
    def _():
        up_copy(quad).wait_recv()
        grad[mine, :] += up_in[quad].astype(F32)

    @pl.when(quad < quads - 1)
    def _():
        down_copy(quad).wait_recv()
        grad[mine, :] += down_in[quad].astype(F32)

    total = grad[mine, :]
    scaled = total * lax.rsqrt(jnp.mean(total * total, axis=-1, keepdims=True) + EPS)
    first = quad * piece
    block = math.gcd(piece, width)
    for part in range(piece // block):
        start = first + part * block
        old = weights_ref[
            head, start // width, pl.ds(pl.multiple_of(start % width, block), block), :
        ]
        fresh_ref[quad, part * block : (part + 1) * block, :] = (
            old.astype(F32) - steps_ref[head] * scaled[part * block : (part + 1) * block, :]
        ).astype(BF16)

    def spread_copy(way, index):
        return remote(
            fresh_ref.at[index],
            fresh_ref.at[index],
            spread_send.at[way, index],
            spread_recv.at[index],
            me + heads if way == 0 else me - heads,
        )

    @pl.when(quad < quads - 1)
    def _():
        spread_copy(0, quad).start()

    @pl.when(quad > 0)
    def _():
        spread_copy(1, quad).start()

    for hop in range(1, quads):

        @pl.when(quad - hop >= 0)
        def _():
            index = quad - hop
            spread_copy(0, index).wait_recv()

            @pl.when(quad < quads - 1)
            def _():
                spread_copy(0, index).start()

        @pl.when(quad + hop < quads)
        def _():
            index = quad + hop
            spread_copy(1, index).wait_recv()

            @pl.when(quad > 0)
            def _():
                spread_copy(1, index).start()

    for step in range(1, n):
        meta_copy(step).wait()
        block_copy(step).wait()
    lane_source, lane_view, lane_slot = (lanes_ref[i : i + 1, :] for i in range(3))
    lane_count = lanes_ref.shape[1]
    counts = got_meta_ref[:, 0, :].astype(BF16)
    sources = lax.broadcasted_iota(jnp.int32, (n, lane_count), 0)
    over_source = (((0,), (0,)), ((), ()))
    same = (sources == lane_source).astype(F32).astype(BF16)
    lower = (sources < lane_source).astype(F32).astype(BF16)
    owners = lax.broadcasted_iota(jnp.int32, (meta_ref.shape[1], lane_count), 0)
    wanted = owners == lane_view + quad * heads

    def lane_sum(table):
        found = lax.dot_general(counts, table, over_source, preferred_element_type=F32)
        return jnp.sum(jnp.where(wanted, found, 0.0), axis=0, keepdims=True).astype(jnp.int32)

    place_at = jnp.where(
        lane_slot < lane_sum(same), lane_view * rows + lane_sum(lower) + lane_slot, -1
    )
    place = (
        lax.broadcasted_iota(jnp.int32, (heads * rows, lane_count), 0) == place_at
    ).astype(F32).astype(BF16)
    arranged = [
        jnp.dot(
            place, got_ref[:, i].reshape(lane_count, width), preferred_element_type=F32
        ).astype(BF16)
        for i in range(3)
    ]
    for view in range(heads):
        part = slice(view * rows, (view + 1) * rows)
        scores = lax.dot_general(
            arranged[0][part], arranged[1][part], (((1,), (1,)), ((), ())),
            preferred_element_type=F32,
        ) * width ** (-0.5)
        powers = jnp.exp(scores - jnp.max(scores, axis=-1, keepdims=True))
        probs = (powers / jnp.sum(powers, axis=-1, keepdims=True)).astype(BF16)
        attended[part] = jnp.dot(probs, arranged[2][part], preferred_element_type=F32)
    query_rows[...] = arranged[0]

    fresh = fresh_ref[...].reshape(3 * width, width)
    pre_gate = jnp.dot(query_rows[...], fresh[0:width], preferred_element_type=F32)
    pre_up = jnp.dot(query_rows[...], fresh[width : 2 * width], preferred_element_type=F32)
    target_hidden = (pre_gate * jax.nn.sigmoid(pre_gate) * pre_up).astype(BF16)
    fast_out = jnp.dot(target_hidden, fresh[2 * width :], preferred_element_type=F32)
    normed = fast_out * lax.rsqrt(jnp.mean(fast_out * fast_out, axis=-1, keepdims=True) + EPS)
    mixed[...] = (normed + attended[...]).astype(BF16).reshape(mixed.shape)
    own_columns = pl.ds(pl.multiple_of(head * width, width), width)

    def out_copy(step):
        view = (head + step) % heads
        return remote(
            mixed.at[view],
            out_ref.at[:, own_columns],
            out_send.at[step],
            out_recv.at[step],
            quad * heads + view,
        )

    for step in range(1, heads):
        out_copy(step).start()
    out_ref[:, own_columns] = mixed[head]
    for step in range(1, heads):
        out_copy(step).wait()

    core_copy(0).wait_send()
    core_copy(1).wait_send()
    for index in range(quads):
        side_copy(index).wait_send()
    for index in range(quads):

        @pl.when(quad < index)
        def _():
            up_copy(index).wait_send()

        @pl.when(quad > index)
        def _():
            down_copy(index).wait_send()

        @pl.when((index <= quad) & (quad < quads - 1))
        def _():
            spread_copy(0, index).wait_send()

        @pl.when((index >= quad) & (quad > 0))
        def _():
            spread_copy(1, index).wait_send()


def exchange(keys, values, rates, weights, steps, queries, view_keys, view_values, views):
    n = lax.axis_size("tokens")
    heads = weights.shape[0]
    width = weights.shape[-1]
    rows = queries.shape[0]
    quads = n // heads
    piece = 3 * width // quads
    capacity = 2 * rows // n
    slots = heads * capacity
    owner_lanes = -(-n // 128) * 128
    lane = np.arange(n * slots)
    lanes = np.zeros((8, n * slots), np.int32)
    lanes[0] = lane // slots
    lanes[1] = lane % slots // capacity
    lanes[2] = lane % capacity
    vmem = pl.BlockSpec(memory_space=pltpu.VMEM)
    smem = pl.BlockSpec(memory_space=pltpu.SMEM)
    dma = pltpu.SemaphoreType.DMA
    whole = (3 * width, width)
    parts = (quads, piece, width)
    return pl.pallas_call(
        functools.partial(exchange_kernel, n, heads),
        out_shape=jax.ShapeDtypeStruct((rows, heads * width), BF16),
        in_specs=[vmem, vmem, vmem, vmem, smem] + [vmem] * 5,
        out_specs=vmem,
        scratch_shapes=[
            pltpu.VMEM((3, n * capacity, heads * width), BF16),
            pltpu.VMEM((8, owner_lanes), F32),
            pltpu.VMEM(parts, BF16),
            pltpu.VMEM((n, 3, slots, width), BF16),
            pltpu.VMEM((n, 8, owner_lanes), F32),
            pltpu.VMEM((heads * rows, width), BF16),
            pltpu.VMEM((heads * rows, width), F32),
            pltpu.VMEM((heads, rows, width), BF16),
            pltpu.VMEM(whole, F32),
            pltpu.VMEM((2,) + whole, BF16),
            pltpu.VMEM((2,) + whole, BF16),
            pltpu.VMEM(whole, BF16),
            pltpu.VMEM(whole, BF16),
            pltpu.VMEM(parts, BF16),
            pltpu.VMEM(parts, BF16),
            pltpu.VMEM(parts, BF16),
            pltpu.VMEM(parts, BF16),
            dma((n,)),
            dma((n,)),
            dma((n,)),
            dma((n,)),
            dma((2,)),
            dma((2,)),
            dma((quads,)),
            dma((quads,)),
            dma((2, quads)),
            dma((2, quads)),
            dma((2, quads)),
            dma((quads,)),
            dma((heads,)),
            dma((heads,)),
        ],
        compiler_params=pltpu.CompilerParams(
            collective_id=0, has_side_effects=True, vmem_limit_bytes=63 * 1024 * 1024
        ),
    )(keys, values, rates, weights, steps, queries, view_keys, view_values, views, jnp.asarray(lanes))


def on_device(
    update_keys,
    update_values,
    update_rates,
    update_mask,
    fast_weights,
    step_sizes,
    target_queries,
    target_keys,
    target_values,
    target_views,
):
    rates = update_rates * update_mask.astype(F32)[:, None]
    return exchange(
        update_keys,
        update_values,
        rates,
        fast_weights,
        step_sizes,
        target_queries,
        target_keys,
        target_values,
        target_views[None, :],
    )


def solution(mesh):
    rows = P(("groups", "tokens"), None)
    flat = P(("groups", "tokens"))
    return jax.shard_map(
        on_device,
        mesh=mesh,
        in_specs=(rows, rows, rows, flat, P(), P(), rows, rows, rows, flat),
        out_specs=rows,
        check_vma=False,
    )
```
